32 devices in a mesh: parts: 2 (over y), seq: 4 (over z), head: 4 (over x, core).
Axes of the slice: x: 2, y: 2, z: 4, core: 2. Of those that a mesh axis runs over, the one named last changes fastest.
Arguments:
- xs: bfloat16 [8192, 5120], P(('parts', 'seq'), 'head'), parts along dimension 0, may hold values from -70 to 70
- gate_in: bfloat16 [8192, 5120], P(('parts', 'seq'), 'head'), parts along dimension 0, may hold values from -6 to 6
- bc_in: bfloat16 [8192, 256], P(('parts', 'seq')), parts along dimension 0, may hold values from -6 to 6
- dt_in: bfloat16 [8192, 64], P(('parts', 'seq'), 'head'), parts along dimension 0, may hold values from -3 to 3
- placement: int32 [8192], P(('parts', 'seq')), parts along dimension 0, may hold values from 0 to 4095, as said below
- lengths: int32 [6], P('parts'), parts along dimension 0, may hold values from 1 to 3072, 4096 in all
- conv_x: float32 [4, 5120], P(None, 'head'), may hold values from -3 to 3
- conv_bc: float32 [4, 256], replicated, may hold values from -3 to 3
- a_log: float32 [64], P('head'), may hold values from -9.5 to -0.5
- dt_bias: float32 [64], P('head'), may hold values from -3 to -1
- d_skip: float32 [64], P('head'), may hold values from 0.3 to 3
- norm_gain: float32 [5120], P('head'), may hold values from 0.1 to 1.9
Outputs:
- mixed: bfloat16 [8192, 5120], P(('parts', 'seq'), 'head'), parts along dimension 0
The draws below stay inside these ranges and needn't reach their ends.
There are 2 independent parts, one for each index of `parts`. The reference program is written for one: setup_inputs(seed, part) draws one part's arguments, and reference() takes and returns one part's arrays. A program takes and returns all parts, laid end to end along the dimension named above; an argument that names none is the same for every part. Nothing has to cross between parts.
Inputs may be any that keep to these rules, and one draw needn't show every extreme that they name: `placement`: A permutation of the packed positions; each ingest device holds exactly 1024 // 4 rows bound for every sequence shard. The lengths sum to 4096; the longest is 3072.
All inputs are finite; a program needn't handle non-finite values.
Results may differ from the reference program's by a relative error of at most 0.0025.
The reference program's roundings to bfloat16 on the way (of `convolved`) count: a program that leaves them out, or rounds other values in their place, can miss the bound.
Values may be sent and summed in bfloat16 or wider, within the bound.
A program may use at most 128 MiB of HBM per device.

```python
import math
import jax
import jax.numpy as jnp
import numpy as np
from jax import lax

HEADS = 64
HEAD_DIM = 80
STATE = 128
KCONV = 4
BLOCK = 256
SEQS = 3
TOK_DEV = 1024
INNER = 5120
TOKENS = 4096


def draw_placement(key, part):
    shard_count = TOKENS // TOK_DEV
    share = TOK_DEV // shard_count
    first_keys = jax.random.split(jax.random.fold_in(key, 11), shard_count)
    orders = jax.vmap(lambda single: jax.random.permutation(single, TOK_DEV))(first_keys)
    slots = orders.astype(jnp.int32) + (jnp.arange(shard_count, dtype=jnp.int32) * TOK_DEV)[:, None]
    slots = slots.reshape(shard_count, shard_count, share).transpose(1, 0, 2).reshape(shard_count, TOK_DEV)
    second_keys = jax.random.split(jax.random.fold_in(key, 12), shard_count)
    shuffles = jax.vmap(lambda single: jax.random.permutation(single, TOK_DEV))(second_keys)
    slots = jnp.take_along_axis(slots, shuffles.astype(jnp.int32), axis=1)
    return slots.reshape(-1).astype(jnp.int32)


def draw_xs(key, part):
    columns = jnp.arange(INNER, dtype=jnp.float32) / INNER
    scales = 0.5 * jnp.power(10.0, columns)
    values = jnp.clip(jax.random.normal(key, (TOKENS, INNER), jnp.float32), -6.0, 6.0)
    return (values * scales[None, :]).astype(jnp.bfloat16)


def draw_a_log(key, part):
    return jax.random.uniform(key, (HEADS,), jnp.float32, -9.5, -0.5)


def level_of(rng, dims, cuts, least, largest):
    loudness, own = 1.0, jax.random.fold_in(rng, 6)
    for dim, shards_of in cuts:
        draws = jnp.exp(jax.random.uniform(jax.random.fold_in(own, dim), (shards_of,), jnp.float32, least / len(cuts), largest / len(cuts)))
        loudness = loudness * jnp.repeat(draws, dims[dim] // shards_of).reshape([-1 if axis == dim else 1 for axis in range(len(dims))])
    return loudness


def profile(amount, total, reach, slope):
    weights = [(1 << 20) // math.isqrt(grade ** slope) + 1 for grade in range(2, amount + 1)]
    rest, counts = total - reach - (amount - 1), [1] * (amount - 1)
    while rest > 0:
        movable = [i for i in range(amount - 1) if counts[i] < reach]
        whole, remaining = sum([weights[i] for i in movable]), rest
        for i in movable:
            extra = min(reach - counts[i], max(1, remaining * weights[i] // whole), rest)
            counts[i] = counts[i] + extra
            rest = rest - extra
    return np.array([reach] + counts)


def ragged(key, number_of, total, limit, slope):
    if number_of == 2:
        one = jax.random.randint(key, (), max(1, total - limit), min(limit, total - 1) + 1)
        return jnp.stack([one, total - one])
    sizes = jnp.asarray(profile(number_of, total, limit, slope), jnp.int32)
    twos = (number_of - 1) // 2
    giver, taker = sizes[1:1 + 2 * twos:2], sizes[2:2 + 2 * twos:2]
    margin = jnp.minimum(giver - 1, limit - taker)
    passed = jax.random.randint(jax.random.fold_in(key, 1), (twos,), 0, 1 << 20) % (margin + 1)
    sizes = sizes.at[1:1 + 2 * twos:2].set(giver - passed).at[2:2 + 2 * twos:2].set(taker + passed)
    return sizes[jax.random.permutation(jax.random.fold_in(key, 2), number_of)]


def centred(own_key, dims, scale, bound, shards=(), held_as=jnp.bfloat16):
    values = jax.random.normal(own_key, dims, jnp.float32) * scale
    if len(shards) > 0:
        values = level_of(own_key, dims, shards, -0.22, 0.18) * values
    return jnp.clip(values, min=-bound, max=bound).astype(held_as)


def setup_inputs(seed: int = 0, part: int = 0) -> dict:
    arg_keys = jax.random.split(jax.random.key(seed), 13)
    part_splits = jax.random.split(jax.random.fold_in(arg_keys[12], part), 13)
    return {
        "xs": draw_xs(jax.random.fold_in(jax.random.fold_in(arg_keys[12], part), 71), part),
        "gate_in": centred(part_splits[1], (TOKENS, INNER), 1.0, 6.0, ((0, 4), (1, 4))),
        "bc_in": centred(part_splits[2], (TOKENS, 2 * STATE), 1.0, 6.0, ((0, 4),)),
        "dt_in": centred(part_splits[3], (TOKENS, HEADS), 0.5, 3.0, ((0, 4), (1, 4))),
        "placement": draw_placement(jax.random.fold_in(jax.random.fold_in(arg_keys[12], part), 71), part),
        "lengths": ragged(part_splits[5], SEQS, TOKENS, 3 * TOKENS // 4, 2).astype(jnp.int32),
        "conv_x": centred(arg_keys[6], (KCONV, INNER), 0.5, 3.0, ((1, 4),), jnp.float32),
        "conv_bc": centred(arg_keys[7], (KCONV, 2 * STATE), 0.5, 3.0, (), jnp.float32),
        "a_log": draw_a_log(jax.random.fold_in(arg_keys[12], 71), part),
        "dt_bias": jnp.clip(-3.0 + 2.0 * jax.random.uniform(arg_keys[9], (HEADS,), jnp.float32) ** level_of(arg_keys[9], (HEADS,), ((0, 4),), -0.2, 0.2), -3.0, -1.0),
        "d_skip": jnp.clip(jnp.exp(math.log(3.0) - 2.3025851 * jax.random.uniform(arg_keys[10], (HEADS,), jnp.float32) ** level_of(arg_keys[10], (HEADS,), ((0, 4),), -0.2, 0.2)), 0.3, 3.0),
        "norm_gain": jnp.clip(1.0 + 0.18 * jax.random.normal(arg_keys[11], (INNER,), jnp.float32), 0.1, 1.9),
    }


highest = lax.Precision.HIGHEST

def convolve(rows, docs_rows, kernel):
    width = kernel.shape[0]
    count = rows.shape[0] - (width - 1)
    total = jnp.zeros((count, rows.shape[1]), jnp.float32)
    for lag in range(width):
        lower = width - 1 - lag
        match = (docs_rows[lower:lower + count] == docs_rows[width - 1:]).astype(jnp.float32)
        total = total + kernel[lag][None, :] * rows[lower:lower + count].astype(jnp.float32) * match[:, None]
    return jax.nn.silu(total).astype(jnp.bfloat16)

def block_pass(carry_state, pieces):
    conv_rows, key_rows, query_rows, step_sizes, log_decay, begins = pieces
    length = step_sizes.shape[0]
    head_count = step_sizes.shape[1]
    log_sums = jnp.cumsum(log_decay, axis=0)
    resets = jnp.cumsum(begins)
    places = jnp.arange(length)
    linked = (places[:, None] >= places[None, :]) & (resets[:, None] == resets[None, :])
    log_gaps = log_sums[:, None, :] - log_sums[None, :, :]
    weights = jnp.exp(jnp.where(linked[:, :, None], log_gaps, -jnp.inf))
    scores = jnp.dot(query_rows, key_rows.T, preferred_element_type=jnp.float32)
    mixing = scores[:, :, None] * weights * step_sizes[None, :, :]
    inputs = conv_rows.astype(jnp.float32).reshape(length, head_count, -1)
    outputs = jnp.einsum('tsh,shp->thp', mixing, inputs, precision=highest)
    carried = jnp.where((resets == 0)[:, None], jnp.exp(log_sums), 0.0)
    queries = query_rows.astype(jnp.float32)
    outputs = outputs + carried[:, :, None] * jnp.einsum('tn,hpn->thp', queries, carry_state, precision=highest)
    closing = jnp.where((resets == resets[-1])[:, None], jnp.exp(log_sums[-1][None, :] - log_sums), 0.0) * step_sizes
    key_values = key_rows.astype(jnp.float32)
    carry_state = carried[-1][:, None, None] * carry_state + jnp.einsum('sh,shp,sn->hpn', closing, inputs, key_values, precision=highest)
    return (carry_state, outputs.reshape(length, -1))

def reference(xs, gate_in, bc_in, dt_in, placement, lengths, conv_x, conv_bc, a_log, dt_bias, d_skip, norm_gain):
    packed_x = jnp.zeros_like(xs).at[placement].set(xs)
    packed_gate = jnp.zeros_like(gate_in).at[placement].set(gate_in)
    packed_bc = jnp.zeros_like(bc_in).at[placement].set(bc_in)
    packed_dt = jnp.zeros_like(dt_in).at[placement].set(dt_in)
    starts = (jnp.cumsum(lengths) - lengths).astype(jnp.int32)
    positions = jnp.arange(TOKENS + KCONV - 1, dtype=jnp.int32) - (KCONV - 1)
    docs = lax.optimization_barrier(jnp.sum((starts[None, :] <= positions[:, None]).astype(jnp.int32), axis=1)) - 1
    begin_all = lax.optimization_barrier(jnp.sum((starts[None, :] == positions[KCONV - 1:, None]).astype(jnp.int32), axis=1))
    channels = jnp.concatenate([packed_x, packed_bc], 1)
    padded = jnp.concatenate([jnp.zeros((KCONV - 1, channels.shape[1]), channels.dtype), channels], 0)
    kernel = jnp.concatenate([conv_x, conv_bc], 1)
    step_all = jax.nn.softplus(packed_dt.astype(jnp.float32) + dt_bias[None, :])
    decay_all = -jnp.exp(a_log)[None, :] * step_all

    def one_block(carry_state, block):
        first = (block * BLOCK).astype(jnp.int32)
        rows = lax.dynamic_slice_in_dim(padded, first, BLOCK + KCONV - 1, 0)
        docs_rows = lax.dynamic_slice_in_dim(docs, first, BLOCK + KCONV - 1, 0)
        convolved = convolve(rows, docs_rows, kernel)
        conv_rows = convolved[:, :INNER]
        key_rows = convolved[:, INNER:INNER + STATE]
        query_rows = convolved[:, INNER + STATE:]
        step_sizes = lax.dynamic_slice_in_dim(step_all, first, BLOCK, 0)
        log_decay = lax.dynamic_slice_in_dim(decay_all, first, BLOCK, 0)
        begins = lax.dynamic_slice_in_dim(begin_all, first, BLOCK, 0)
        carry_state, outputs = block_pass(carry_state, (conv_rows, key_rows, query_rows, step_sizes, log_decay, begins))
        inputs = conv_rows.astype(jnp.float32).reshape(BLOCK, HEADS, HEAD_DIM)
        outputs = outputs + (d_skip[None, :, None] * inputs).reshape(BLOCK, INNER)
        gates = lax.dynamic_slice_in_dim(packed_gate, first, BLOCK, 0)
        gated = outputs * jax.nn.silu(gates.astype(jnp.float32))
        mean_square = lax.optimization_barrier(jnp.sum(gated * gated, axis=1)) / INNER
        result = gated * lax.rsqrt(mean_square + 1e-05)[:, None] * norm_gain[None, :]
        return (carry_state, result.astype(jnp.bfloat16))
    empty = jnp.zeros((HEADS, HEAD_DIM, STATE), jnp.float32)
    blocks = jnp.arange(TOKENS // BLOCK, dtype=jnp.int32)
    final_state, results = lax.scan(one_block, empty, blocks)
    return results.reshape(TOKENS, INNER)
```

```python
import functools

import jax
import jax.numpy as jnp
from jax import lax
from jax.experimental import pallas as pl
from jax.experimental.pallas import tpu as pltpu
from jax.sharding import PartitionSpec as P

BLOCK = 256
LANES = 128
RIM = 8
HIGHEST = lax.Precision.HIGHEST
F32 = jnp.float32
BF16 = jnp.bfloat16


def iota(shape, dim):
    return lax.broadcasted_iota(jnp.int32, shape, dim)


def dot(a, b, dims=((1,), (0,))):
    return lax.dot_general(a, b, (dims, ((), ())), preferred_element_type=F32)


def halves(value):
    high = value.astype(BF16)
    return high, (value - high.astype(F32)).astype(BF16)


def dot_left(a, b):
    high, low = halves(a)
    return dot(high, b) + dot(low, b)


def dot_right(a, b, dims=((1,), (0,))):
    high, low = halves(b)
    return dot(a, high, dims) + dot(a, low, dims)


def spread(head_dim, width):
    head, channel = iota((LANES, width), 0), iota((LANES, width), 1)
    inside = (channel >= head * head_dim) & (channel < (head + 1) * head_dim)
    return inside.astype(F32).astype(BF16)


def send_kernel(shards, per, rim, width, place_ref, *refs):
    ins, (out_ref, slot_ref) = refs[:-2], refs[-2:]
    rows = place_ref.shape[1]
    dest = pl.program_id(0)
    place = place_ref[0:1, :]
    target = lax.shift_right_logical(place, rows.bit_length() - 1)

    @pl.when(dest == 0)
    def _():
        groups = -(-shards // 16) * 16
        chosen = iota((groups, rows), 0) == target
        before = (iota((rows, rows), 0) < iota((rows, rows), 1)).astype(F32).astype(BF16)
        counts = dot(chosen.astype(F32).astype(BF16), before)
        slot = jnp.sum(jnp.where(chosen, counts, 0.0), axis=0, keepdims=True)
        slot_ref[...] = jnp.broadcast_to(slot.astype(jnp.int32), slot_ref.shape)

    offset = place - dest * rows
    key = jnp.where(target == dest, slot_ref[0:1, :], -1)
    if rim:
        key = jnp.where((offset < 0) & (offset >= 1 - width), offset + (width - 1 + per), key)
    pick = (iota((per + rim, rows), 0) == key).astype(F32).astype(BF16)
    column = 0
    for ref in ins:
        count = ref.shape[1]
        out_ref[0, :, column : column + count] = dot(pick, ref[...]).astype(BF16)
        column += count


def send_rows(place, arrays, shards, rim, width):
    rows = place.shape[1]
    per = rows // shards
    columns = sum(array.shape[1] for array in arrays)
    return pl.pallas_call(
        functools.partial(send_kernel, shards, per, rim, width),
        grid=(shards,),
        in_specs=[pl.BlockSpec(place.shape, lambda k: (0, 0))]
        + [pl.BlockSpec(array.shape, lambda k: (0, 0)) for array in arrays],
        out_specs=pl.BlockSpec((1, per + rim, columns), lambda k: (k, 0, 0)),
        out_shape=jax.ShapeDtypeStruct((shards, per + rim, columns), BF16),
        scratch_shapes=[pltpu.VMEM((8, rows), jnp.int32)],
        cost_estimate=pl.CostEstimate(
            flops=2 * rows * rows * columns, bytes_accessed=4 * rows * columns, transcendentals=0
        ),
    )(place, *arrays)


def doc_at(start_ref, position):
    total = jnp.where(start_ref[0] <= position, 1, 0)
    for j in range(1, start_ref.shape[0] - 1):
        total = total + jnp.where(start_ref[j] <= position, 1, 0)
    return total


def scan_kernel(
    per, heads, start_ref, arrived_ref, taps_ref, head_ref, skip_ref,
    y_ref, query_ref, carry_ref, slot_ref, state_ref, total_ref,
):
    chunk = pl.program_id(0)
    width = taps_ref.shape[0]
    inner = y_ref.shape[1]
    head_dim = inner // heads
    mixed = inner + 2 * LANES
    rows_in = arrived_ref.shape[0]
    base = start_ref[start_ref.shape[0] - 1]
    origin = base + chunk * BLOCK

    @pl.when(chunk == 0)
    def _():
        tail = arrived_ref[:, mixed : mixed + LANES]
        lane, row = iota((16, LANES), 1), iota((16, LANES), 0)
        factor = jnp.where(lane == heads, 32.0, jnp.where(lane == heads + 1, 1.0, 0.0))
        factor = jnp.where(row == 0, factor, 0.0).astype(BF16)
        place = dot(factor, tail, ((1,), (1,)))[0:8, :].astype(jnp.int32)
        within = iota((8, rows_in), 1) % (per + RIM)
        slot_ref[...] = jnp.where(within >= per, place - pl.num_programs(0) * BLOCK, place)
        state_ref[...] = jnp.zeros_like(state_ref)
        total_ref[...] = jnp.zeros_like(total_ref)

    wanted = iota((BLOCK + RIM, rows_in), 0) + (chunk * BLOCK - RIM)
    pick = (wanted == slot_ref[0:1, :]).astype(F32).astype(BF16)
    column = iota((BLOCK, 1), 0) + origin
    docs = doc_at(start_ref, column)
    matches = [None] + [
        (doc_at(start_ref, column - lag) == docs) & (column >= lag) for lag in range(1, width)
    ]

    def convolved(first, count):
        packed = dot(pick, arrived_ref[:, first : first + count])
        total = taps_ref[0:1, first : first + count] * packed[RIM:, :]
        for lag in range(1, width):
            part = taps_ref[lag : lag + 1, first : first + count] * packed[RIM - lag : RIM - lag + BLOCK, :]
            total = total + jnp.where(matches[lag], part, 0.0)
        return (total * jax.nn.sigmoid(total)).astype(BF16)

    x = convolved(0, inner)
    keys = convolved(inner, LANES)
    query = convolved(inner + LANES, LANES)
    query_ref[...] = query
    raw = dot(pick, arrived_ref[:, mixed : mixed + LANES])[RIM:, :]
    raw = raw + head_ref[1:2, :]
    lane = iota((1, LANES), 1)
    step = jnp.maximum(raw, 0.0) + jnp.log1p(jnp.exp(-jnp.abs(raw)))
    step = jnp.where(lane < heads, step, 0.0)
    rate = jnp.exp(head_ref[0:1, :])
    decay = -rate * step
    lower = iota((BLOCK, BLOCK), 0) >= iota((BLOCK, BLOCK), 1)
    sums = jnp.dot(lower.astype(F32), decay, precision=HIGHEST, preferred_element_type=F32)
    sums_t = sums.T
    step_t = step.T
    docs_row = doc_at(start_ref, iota((1, BLOCK), 1) + origin)
    linked = lower & (docs == docs_row)
    scores = jnp.where(linked, dot(query, keys, ((1,), (1,))), 0.0)
    doc_before = doc_at(start_ref, origin - 1)
    doc_before = jnp.where(origin > 0, doc_before, 0)
    doc_base = jnp.where(base > 0, doc_at(start_ref, base - 1), 0)
    doc_last = doc_at(start_ref, origin + BLOCK - 1)
    carried = jnp.where(docs == doc_before, jnp.exp(sums), 0.0)
    last = sums[BLOCK - 1 : BLOCK, :]
    closing = jnp.where(docs == doc_last, jnp.exp(jnp.minimum(last - sums, 0.0)), 0.0) * step
    before = total_ref[0:1, :]
    carry_ref[...] = jnp.where(docs == doc_base, jnp.exp(before + sums), 0.0)
    total_ref[...] = jnp.broadcast_to(before + last, total_ref.shape)

    expand = spread(head_dim, inner)
    carried_all = dot_left(carried, expand)
    state = state_ref[...]
    x32 = x.astype(F32)
    y_ref[...] = carried_all * dot_right(query, state) + skip_ref[0:1, :] * x32
    weighted = dot_left(closing, expand) * x32
    state_ref[...] = carried_all[BLOCK - 1 : BLOCK, :] * state + dot_right(keys, weighted, ((0,), (0,)))

    for head in range(heads):
        first, end = head * head_dim, (head + 1) * head_dim
        low, high = first // LANES * LANES, -(-end // LANES) * LANES
        gap = sums[:, head : head + 1] - sums_t[head : head + 1, :]
        weight = jnp.exp(jnp.minimum(gap, 0.0)) * step_t[head : head + 1, :] * scores
        channel = iota((1, high - low), 1) + low
        own = jnp.where((channel >= first) & (channel < end), x32[:, low:high], 0.0).astype(BF16)
        y_ref[:, low:high] += dot_left(weight, own)


def scan_blocks(starts, arrived, taps, head_rows, skip, per, heads, rows):
    rows_in, columns = arrived.shape
    inner = skip.shape[1]
    fixed = lambda shape: pl.BlockSpec(shape, lambda c: (0, 0))
    return pl.pallas_call(
        functools.partial(scan_kernel, per, heads),
        grid=(rows // BLOCK,),
        in_specs=[
            pl.BlockSpec(memory_space=pltpu.SMEM),
            fixed(arrived.shape),
            fixed(taps.shape),
            fixed(head_rows.shape),
            fixed(skip.shape),
        ],
        out_specs=[
            pl.BlockSpec((BLOCK, inner), lambda c: (c, 0)),
            pl.BlockSpec((BLOCK, LANES), lambda c: (c, 0)),
            pl.BlockSpec((BLOCK, LANES), lambda c: (c, 0)),
            fixed((8, rows_in)),
            fixed((LANES, inner)),
        ],
        out_shape=[
            jax.ShapeDtypeStruct((rows, inner), F32),
            jax.ShapeDtypeStruct((rows, LANES), BF16),
            jax.ShapeDtypeStruct((rows, LANES), F32),
            jax.ShapeDtypeStruct((8, rows_in), jnp.int32),
            jax.ShapeDtypeStruct((LANES, inner), F32),
        ],
        scratch_shapes=[pltpu.VMEM((8, LANES), F32)],
        compiler_params=pltpu.CompilerParams(vmem_limit_bytes=56 << 20),
        cost_estimate=pl.CostEstimate(
            flops=20_000_000_000, bytes_accessed=12_000_000, transcendentals=rows * BLOCK * heads
        ),
    )(starts, arrived, taps, head_rows, skip)


def gate_kernel(heads, gate_ref, slot_ref, y_ref, query_ref, carry_ref, state_ref, out_ref, square_ref):
    chunk = pl.program_id(0)
    inner = y_ref.shape[1]
    rows_in = gate_ref.shape[0]
    pick = (iota((BLOCK, rows_in), 0) + chunk * BLOCK == slot_ref[0:1, :]).astype(F32).astype(BF16)
    gate = dot(pick, gate_ref[...])
    expand = spread(inner // heads, inner)
    y = y_ref[...] + dot_left(carry_ref[...], expand) * dot_right(query_ref[...], state_ref[...])
    gated = y * (gate * jax.nn.sigmoid(gate))
    out_ref[...] = gated
    squares = jnp.sum(gated * gated, axis=1, keepdims=True)
    square_ref[...] = jnp.broadcast_to(squares, (BLOCK, LANES)).T[0:8, :]


def gate_rows(gate, slots, y, query, carry, state, heads):
    rows, inner = y.shape
    fixed = lambda array: pl.BlockSpec(array.shape, lambda c: (0, 0))
    tiled = lambda array: pl.BlockSpec((BLOCK, array.shape[1]), lambda c: (c, 0))
    return pl.pallas_call(
        functools.partial(gate_kernel, heads),
        grid=(rows // BLOCK,),
        in_specs=[fixed(gate), fixed(slots), tiled(y), tiled(query), tiled(carry), fixed(state)],
        out_specs=[
            pl.BlockSpec((BLOCK, inner), lambda c: (c, 0)),
            pl.BlockSpec((8, BLOCK), lambda c: (0, c)),
        ],
        out_shape=[
            jax.ShapeDtypeStruct((rows, inner), F32),
            jax.ShapeDtypeStruct((8, rows), F32),
        ],
        cost_estimate=pl.CostEstimate(
            flops=5_000_000_000, bytes_accessed=16_000_000, transcendentals=rows * inner
        ),
    )(gate, slots, y, query, carry, state)


def body(
    xs, gate_in, bc_in, dt_in, placement, lengths,
    conv_x, conv_bc, a_log, dt_bias, d_skip, norm_gain, *, full_inner,
):
    shards = lax.axis_size("seq")
    mine = lax.axis_index("seq")
    rows, inner = xs.shape
    heads = a_log.shape[0]
    head_dim = inner // heads
    per = rows // shards
    width = conv_x.shape[0]
    place = jnp.broadcast_to(placement[None, :], (8, rows))
    local = placement % rows
    digits = jnp.stack([local // 32, local % 32], 1).astype(BF16)
    spare = jnp.zeros((rows, LANES - heads - 2), BF16)
    small = jnp.concatenate([bc_in, dt_in, digits, spare], 1)
    sent = send_rows(place, (xs, small), shards, RIM, width)
    arrived = lax.all_to_all(sent, "seq", split_axis=0, concat_axis=0, tiled=True)
    gate_sent = send_rows(place, (gate_in,), shards, 0, width)
    arrived, gate_sent = lax.optimization_barrier((arrived, gate_sent))
    gate = lax.all_to_all(gate_sent, "seq", split_axis=0, concat_axis=0, tiled=True)

    starts = jnp.concatenate(
        [jnp.cumsum(lengths) - lengths, jnp.asarray(mine * rows, jnp.int32)[None]]
    )
    taps = jnp.concatenate([conv_x, conv_bc], 1)
    head_rows = jnp.zeros((8, LANES), F32).at[0, :heads].set(a_log).at[1, :heads].set(dt_bias)
    skip = jnp.broadcast_to(jnp.repeat(d_skip, head_dim)[None, :], (8, inner))
    y, query, carry, slots, state = scan_blocks(
        starts, arrived.reshape(shards * (per + RIM), -1), taps, head_rows, skip, per, heads, rows
    )
    keep = jnp.repeat(carry[rows - 1, :heads], head_dim)[None, :]
    incoming = jnp.zeros_like(state)
    for hop in range(1, shards):
        onward = (keep * incoming + state).astype(BF16)
        came = lax.ppermute(onward, "seq", [(hop - 1, hop)])
        incoming = jnp.where(mine == hop, came.astype(F32), incoming)
    gate_slots = slots.reshape(8, shards, per + RIM)[:, :, :per].reshape(8, rows)
    gated, squares = gate_rows(
        gate.reshape(rows, inner), gate_slots, y, query, carry, incoming, heads
    )
    squares = lax.psum(squares[0], "head")
    result = gated * lax.rsqrt(squares / full_inner + 1e-05)[:, None] * norm_gain[None, :]
    return result.astype(BF16)


def solution(mesh):
    in_specs = (
        P(("parts", "seq"), "head"),
        P(("parts", "seq"), "head"),
        P(("parts", "seq"), None),
        P(("parts", "seq"), "head"),
        P(("parts", "seq")),
        P("parts"),
        P(None, "head"),
        P(),
        P("head"),
        P("head"),
        P("head"),
        P("head"),
    )
    out_specs = P(("parts", "seq"), "head")

    def whole(*args):
        step = functools.partial(body, full_inner=args[0].shape[1])
        return jax.shard_map(
            step, mesh=mesh, in_specs=in_specs, out_specs=out_specs, check_vma=False
        )(*args)

    return whole
```

```python
import functools

import jax
import jax.numpy as jnp
from jax import lax
from jax.experimental import pallas as pl
from jax.experimental.pallas import tpu as pltpu
from jax.sharding import PartitionSpec as P

BLOCK = 256
LANES = 128
RIM = 8
HIGHEST = lax.Precision.HIGHEST
MESH = pl.DeviceIdType.MESH
F32 = jnp.float32
BF16 = jnp.bfloat16


def iota(shape, dim):
    return lax.broadcasted_iota(jnp.int32, shape, dim)


def dot(a, b, dims=((1,), (0,))):
    return lax.dot_general(a, b, (dims, ((), ())), preferred_element_type=F32)


def halves(value):
    high = value.astype(BF16)
    return high, (value - high.astype(F32)).astype(BF16)


def dot_left(a, b):
    high, low = halves(a)
    return dot(high, b) + dot(low, b)


def dot_right(a, b):
    high, low = halves(b)
    return dot(jnp.concatenate([a, a], 1), jnp.concatenate([high, low], 0))


def dot_turned(a, b):
    high, low = halves(b)
    dims = ((0,), (0,))
    return dot(a, high, dims) + dot(a, low, dims)


def expanded(value, heads, head_dim, width):
    head, channel = iota((LANES, width), 0), iota((LANES, width), 1)
    head = jnp.where(head < heads, head, head - LANES // 2)
    inside = (channel >= head * head_dim) & (channel < (head + 1) * head_dim)
    high, low = halves(value)
    low = pltpu.roll(low.astype(F32), LANES // 2, 1)
    lane = iota((1, LANES), 1)
    both = jnp.where(lane < LANES // 2, high.astype(F32), low)
    return dot(both.astype(BF16), inside.astype(F32).astype(BF16))


def picked(place, slot, dest, per, rim, width):
    rows = place.shape[1]
    target = lax.shift_right_logical(place, rows.bit_length() - 1)
    offset = place - dest * rows
    key = jnp.where(target == dest, slot, -1)
    if rim:
        key = jnp.where((offset < 0) & (offset >= 1 - width), offset + (width - 1 + per), key)
    return (iota((per + rim, rows), 0) == key).astype(F32).astype(BF16)


def greet(axes):
    barrier = pltpu.get_barrier_semaphore()
    for axis in axes:
        count, me = lax.axis_size(axis), lax.axis_index(axis)

        def signal(i, _, axis=axis, count=count, me=me):
            pl.semaphore_signal(
                barrier, inc=1, device_id={axis: lax.rem(me + i, count)}, device_id_type=MESH
            )
            return 0

        lax.fori_loop(1, count, signal, 0)
    pl.semaphore_wait(barrier, sum(lax.axis_size(axis) - 1 for axis in axes))


def remote(source, target, sends, receives, axis, offset):
    count, me = lax.axis_size(axis), lax.axis_index(axis)
    return pltpu.make_async_remote_copy(
        src_ref=source,
        dst_ref=target,
        send_sem=sends,
        recv_sem=receives,
        device_id={axis: lax.rem(me + offset, count)},
        device_id_type=MESH,
    )


def move_kernel(
    width, heads, place_ref, x_ref, small_ref, gate_ref, arrived_ref, tails_ref, gate_out_ref,
    x_send, small_send, x_sems, small_sems, tail_sems,
):
    shards, peers = lax.axis_size("seq"), lax.axis_size("head")
    me, own = lax.axis_index("seq"), lax.axis_index("head")
    rows = place_ref.shape[1]
    per = rows // shards
    greet(("seq", "head"))
    place = place_ref[0:1, :]
    groups = -(-shards // 16) * 16
    target = lax.shift_right_logical(place, rows.bit_length() - 1)
    chosen = iota((groups, rows), 0) == target
    before = (iota((rows, rows), 0) < iota((rows, rows), 1)).astype(F32).astype(BF16)
    counts = dot(chosen.astype(F32).astype(BF16), before)
    slot = jnp.sum(jnp.where(chosen, counts, 0.0), axis=0, keepdims=True).astype(jnp.int32)
    local = place & (rows - 1)
    line = iota((LANES, rows), 0)
    digits = jnp.where(line == heads, local >> 5, jnp.where(line == heads + 1, local & 31, 0))
    digits = digits.astype(F32).astype(BF16)

    def x_copy(i):
        return remote(
            x_send.at[i], arrived_ref.at[me], x_sems.at[0, i], x_sems.at[1, i], "seq", i
        )

    def small_copy(i):
        return remote(
            small_send.at[i], tails_ref.at[own, me], small_sems.at[0, i], small_sems.at[1, i], "seq", i
        )

    def tail_copy(i):
        return remote(
            tails_ref.at[own], tails_ref.at[own], tail_sems.at[0, i], tail_sems.at[1, i], "head", i
        )

    def small_step(i, _):
        pick = picked(place, slot, lax.rem(me + i, shards), per, RIM, width)
        values = dot(pick, small_ref[...]) + dot(pick, digits, ((1,), (1,)))
        small_send[i] = values.astype(BF16)
        return 0

    def x_step(i, _):
        pick = picked(place, slot, lax.rem(me + i, shards), per, RIM, width)
        x_send[i] = dot(pick, x_ref[...]).astype(BF16)

        @pl.when(i > 1)
        def _():
            x_copy(i - 1).start()

        return 0

    def each(first, last, action):
        def step(i, _):
            action(i)
            return 0

        lax.fori_loop(first, last, step, 0)

    lax.fori_loop(0, shards, small_step, 0)
    lax.fori_loop(1, 2, x_step, 0)
    each(1, shards, lambda i: small_copy(i).start())
    lax.fori_loop(2, shards, x_step, 0)
    tails_ref[own, me] = small_send[0]
    pick = picked(place, slot, me, per, RIM, width)
    arrived_ref[me] = dot(pick, x_ref[...]).astype(BF16)
    x_copy(shards - 1).start()

    def gate_step(dest, _):
        pick = picked(place, slot, dest, per, 0, width)
        gate_out_ref[dest] = dot(pick, gate_ref[...]).astype(BF16)
        return 0

    lax.fori_loop(0, shards, gate_step, 0)
    each(1, shards, lambda i: small_copy(i).wait())
    each(1, peers, lambda i: tail_copy(i).start())
    each(1, peers, lambda i: tail_copy(i).wait())
    each(1, shards, lambda i: x_copy(i).wait())


def move_rows(place, xs, small, gate, width, heads):
    shards, peers = lax.axis_size("seq"), lax.axis_size("head")
    rows, inner = xs.shape
    per = rows // shards
    vmem = pl.BlockSpec(memory_space=pltpu.VMEM)
    return pl.pallas_call(
        functools.partial(move_kernel, width, heads),
        in_specs=[vmem] * 4,
        out_specs=[vmem] * 3,
        out_shape=[
            jax.ShapeDtypeStruct((shards, per + RIM, inner), BF16),
            jax.ShapeDtypeStruct((peers, shards, per + RIM, LANES), BF16),
            jax.ShapeDtypeStruct((shards, per, inner), BF16),
        ],
        scratch_shapes=[
            pltpu.VMEM((shards, per + RIM, inner), BF16),
            pltpu.VMEM((shards, per + RIM, LANES), BF16),
            pltpu.SemaphoreType.DMA((2, shards)),
            pltpu.SemaphoreType.DMA((2, shards)),
            pltpu.SemaphoreType.DMA((2, peers)),
        ],
        compiler_params=pltpu.CompilerParams(
            collective_id=0, has_side_effects=True, vmem_limit_bytes=56 << 20
        ),
    )(place, xs, small, gate)


def doc_at(start_ref, position):
    total = jnp.where(start_ref[0] <= position, 1, 0)
    for j in range(1, start_ref.shape[0] - 1):
        total = total + jnp.where(start_ref[j] <= position, 1, 0)
    return total


def scan_step(
    chunk, chunks, per, heads, start_ref, arrived_ref, bc_ref, tail_ref, taps_ref, head_ref,
    skip_ref, y_ref, query_ref, carry_ref, slot_ref, state_ref, total_ref,
):
    width = taps_ref.shape[0]
    inner = y_ref.shape[1]
    head_dim = inner // heads
    rows_in = arrived_ref.shape[0]
    base = start_ref[start_ref.shape[0] - 1]
    origin = base + chunk * BLOCK
    here = pl.ds(pl.multiple_of(chunk * BLOCK, BLOCK), BLOCK)

    wanted = iota((BLOCK + RIM, rows_in), 0) + (chunk * BLOCK - RIM)
    pick = (wanted == slot_ref[0:1, :]).astype(F32).astype(BF16)
    column = iota((BLOCK, 1), 0) + origin
    docs = doc_at(start_ref, column)
    matches = [None] + [
        (doc_at(start_ref, column - lag) == docs) & (column >= lag) for lag in range(1, width)
    ]

    def convolved(packed, first):
        count = packed.shape[1]
        total = taps_ref[0:1, first : first + count] * packed[RIM:, :]
        for lag in range(1, width):
            part = taps_ref[lag : lag + 1, first : first + count] * packed[RIM - lag : RIM - lag + BLOCK, :]
            total = total + jnp.where(matches[lag], part, 0.0)
        return (total * jax.nn.sigmoid(total)).astype(BF16)

    x = convolved(dot(pick, arrived_ref[...]), 0)
    both = convolved(dot(pick, bc_ref[...]), inner)
    keys, query = both[:, :LANES], both[:, LANES:]
    query_ref[here, :] = query
    raw = dot(pick, tail_ref[...])[RIM:, :]
    raw = raw + head_ref[1:2, :]
    lane = iota((1, LANES), 1)
    step = jnp.maximum(raw, 0.0) + jnp.log1p(jnp.exp(-jnp.abs(raw)))
    step = jnp.where(lane < heads, step, 0.0)
    rate = jnp.exp(head_ref[0:1, :])
    decay = -rate * step
    lower = iota((BLOCK, BLOCK), 0) >= iota((BLOCK, BLOCK), 1)
    sums = jnp.dot(lower.astype(F32), decay, precision=HIGHEST, preferred_element_type=F32)
    sums_t = sums.T
    step_t = step.T
    docs_row = doc_at(start_ref, iota((1, BLOCK), 1) + origin)
    linked = lower & (docs == docs_row)
    scores = jnp.where(linked, dot(query, keys, ((1,), (1,))), 0.0)
    doc_before = doc_at(start_ref, origin - 1)
    doc_before = jnp.where(origin > 0, doc_before, 0)
    doc_base = jnp.where(base > 0, doc_at(start_ref, base - 1), 0)
    doc_last = doc_at(start_ref, origin + BLOCK - 1)
    carried = jnp.where(docs == doc_before, jnp.exp(sums), 0.0)
    last = sums[BLOCK - 1 : BLOCK, :]
    closing = jnp.where(docs == doc_last, jnp.exp(jnp.minimum(last - sums, 0.0)), 0.0) * step
    before = total_ref[0:1, :]
    carry_ref[here, :] = jnp.where(docs == doc_base, jnp.exp(before + sums), 0.0)
    total_ref[...] = jnp.broadcast_to(before + last, total_ref.shape)

    carried_all = expanded(carried, heads, head_dim, inner)
    state = state_ref[...]
    x32 = x.astype(F32)
    y_ref[here, :] = carried_all * dot_right(query, state) + skip_ref[0:1, :] * x32
    weighted = expanded(closing, heads, head_dim, inner) * x32
    state_ref[...] = carried_all[BLOCK - 1 : BLOCK, :] * state + dot_turned(keys, weighted)

    for head in range(heads):
        first, end = head * head_dim, (head + 1) * head_dim
        low, high = first // LANES * LANES, -(-end // LANES) * LANES
        gap = sums[:, head : head + 1] - sums_t[head : head + 1, :]
        weight = jnp.exp(jnp.minimum(gap, 0.0)) * step_t[head : head + 1, :] * scores
        channel = iota((1, high - low), 1) + low
        own = jnp.where((channel >= first) & (channel < end), x32[:, low:high], 0.0).astype(BF16)
        y_ref[here, low:high] += dot_left(weight, own)


def start_step(per, heads, tail_ref, slot_ref, gate_slot_ref):
    shards = lax.axis_size("seq")
    block = per + RIM
    lane, row = iota((16, LANES), 1), iota((16, LANES), 0)
    factor = jnp.where(lane == heads, 32.0, jnp.where(lane == heads + 1, 1.0, 0.0))
    factor = jnp.where(row == 0, factor, 0.0).astype(BF16)
    place = dot(factor, tail_ref[...], ((1,), (1,)))[0:8, :].astype(jnp.int32)
    within = iota((8, shards * block), 1) % block
    slot_ref[...] = jnp.where(within >= per, place - per * shards, place)
    for source in range(shards):
        gate_slot_ref[:, source * per : (source + 1) * per] = place[
            :, source * block : source * block + per
        ]


def layer_kernel(
    per, heads, full_inner, start_ref, arrived_ref, bc_ref, tail_ref, taps_ref, head_ref, skip_ref,
    gain_ref, gate_ref, out_ref,
    y_ref, query_ref, carry_ref, slot_ref, gate_slot_ref, state_ref, total_ref,
    gate_in, came, onward, incoming, squares, gate_sems, own_sem, state_sems, square_sems,
):
    shards, peers = lax.axis_size("seq"), lax.axis_size("head")
    me, own = lax.axis_index("seq"), lax.axis_index("head")
    step = pl.program_id(0)
    rows, inner = y_ref.shape
    chunks = rows // BLOCK
    head_dim = inner // heads
    pieces, _, wide = came.shape

    def gate_copy(i):
        to = lax.rem(me + i, shards)
        return remote(
            gate_ref.at[to], gate_in.at[me], gate_sems.at[0, i], gate_sems.at[1, i], "seq", i
        )

    def own_copy():
        return pltpu.make_async_copy(gate_ref.at[me], gate_in.at[me], own_sem)

    def state_copy(piece):
        return remote(
            onward.at[piece], came.at[piece], state_sems.at[0, piece], state_sems.at[1, piece], "seq", 1
        )

    def square_copy(chunk, i):
        return remote(
            squares.at[own, chunk], squares.at[own, chunk],
            square_sems.at[0, chunk, i], square_sems.at[1, chunk, i], "head", i,
        )

    def each(first, last, action):
        def once(i, _):
            action(i)
            return 0

        lax.fori_loop(first, last, once, 0)

    @pl.when(step == 0)
    def _():
        greet(("seq", "head"))
        each(1, shards, lambda i: gate_copy(i).start())
        own_copy().start()
        start_step(per, heads, tail_ref, slot_ref, gate_slot_ref)
        state_ref[...] = jnp.zeros_like(state_ref)
        total_ref[...] = jnp.zeros_like(total_ref)

    @pl.when(step < chunks)
    def _():
        scan_step(
            step, chunks, per, heads, start_ref, arrived_ref, bc_ref, tail_ref, taps_ref, head_ref,
            skip_ref, y_ref, query_ref, carry_ref, slot_ref, state_ref, total_ref,
        )

    @pl.when(step == chunks - 1)
    def _():
        tail_rows = carry_ref[rows - 8 : rows, :]
        keep = expanded(tail_rows, heads, head_dim, inner)[7:8, :]
        for piece in range(pieces):
            span = slice(piece * wide, (piece + 1) * wide)

            @pl.when(me > 0)
            def _():
                state_copy(piece).wait_recv()
                incoming[:, span] = came[piece].astype(F32)

            @pl.when(me == 0)
            def _():
                incoming[:, span] = jnp.zeros((LANES, wide), F32)

            passed = keep[:, span] * incoming[:, span] + state_ref[:, span]
            onward[piece] = passed.astype(BF16)
            if piece > 0:

                @pl.when(me < shards - 1)
                def _():
                    state_copy(piece - 1).start()

        state_ref[...] = incoming[...]

        @pl.when(me < shards - 1)
        def _():
            state_copy(pieces - 1).start()
            for piece in range(pieces):
                state_copy(piece).wait_send()

        each(1, shards, lambda i: gate_copy(i).wait())
        own_copy().wait()

    @pl.when((step > chunks) & (step <= 2 * chunks))
    def _():
        each(1, peers, lambda i: square_copy(step - chunks - 1, i).start())

    @pl.when((step >= chunks) & (step < 2 * chunks))
    def _():
        chunk = step - chunks
        here = pl.ds(pl.multiple_of(chunk * BLOCK, BLOCK), BLOCK)
        wanted = iota((BLOCK, rows), 0) + chunk * BLOCK
        pick = (wanted == gate_slot_ref[0:1, :]).astype(F32).astype(BF16)
        gate = dot(pick, gate_in[...].reshape(rows, inner))
        carried = expanded(carry_ref[here, :], heads, head_dim, inner)
        y = y_ref[here, :] + carried * dot(query_ref[here, :], state_ref[...].astype(BF16))
        gated = y * (gate * jax.nn.sigmoid(gate))
        y_ref[here, :] = gated
        total = jnp.sum(gated * gated, axis=1, keepdims=True)
        squares[own, chunk] = jnp.broadcast_to(total, (BLOCK, LANES)).T[0:8, :]

    @pl.when(step >= 2 * chunks)
    def _():
        chunk = step - 2 * chunks
        here = pl.ds(pl.multiple_of(chunk * BLOCK, BLOCK), BLOCK)
        each(1, peers, lambda i: square_copy(chunk, i).wait())
        total = squares[0, chunk]
        for peer in range(1, peers):
            total = total + squares[peer, chunk]
        scale = lax.rsqrt(total / full_inner + 1e-05)
        scale = jnp.concatenate([scale] * (LANES // 8), 0).T[:, 0:1]
        out_ref[...] = (y_ref[here, :] * scale * gain_ref[0:1, :]).astype(BF16)


def layer(starts, arrived, bc, tail, taps, head_rows, skip, gain, gate, per, heads, rows, full_inner):
    shards, peers = lax.axis_size("seq"), lax.axis_size("head")
    rows_in, inner = arrived.shape
    chunks = rows // BLOCK
    wide = 2 * LANES
    vmem = pl.BlockSpec(memory_space=pltpu.VMEM)
    return pl.pallas_call(
        functools.partial(layer_kernel, per, heads, full_inner),
        grid=(3 * chunks,),
        in_specs=[pl.BlockSpec(memory_space=pltpu.SMEM)]
        + [vmem] * 7
        + [pl.BlockSpec(memory_space=pl.ANY)],
        out_specs=pl.BlockSpec((BLOCK, inner), lambda k: (jnp.maximum(k - 2 * chunks, 0), 0)),
        out_shape=jax.ShapeDtypeStruct((rows, inner), BF16),
        scratch_shapes=[
            pltpu.VMEM((rows, inner), F32),
            pltpu.VMEM((rows, LANES), BF16),
            pltpu.VMEM((rows, LANES), F32),
            pltpu.VMEM((8, rows_in), jnp.int32),
            pltpu.VMEM((8, rows), jnp.int32),
            pltpu.VMEM((LANES, inner), F32),
            pltpu.VMEM((8, LANES), F32),
            pltpu.VMEM((shards, per, inner), BF16),
            pltpu.VMEM((inner // wide, LANES, wide), BF16),
            pltpu.VMEM((inner // wide, LANES, wide), BF16),
            pltpu.VMEM((LANES, inner), F32),
            pltpu.VMEM((peers, chunks, 8, BLOCK), F32),
            pltpu.SemaphoreType.DMA((2, shards)),
            pltpu.SemaphoreType.DMA,
            pltpu.SemaphoreType.DMA((2, inner // wide)),
            pltpu.SemaphoreType.DMA((2, chunks, peers)),
        ],
        compiler_params=pltpu.CompilerParams(
            collective_id=1, has_side_effects=True, vmem_limit_bytes=60 << 20
        ),
    )(starts, arrived, bc, tail, taps, head_rows, skip, gain, gate)


def body(
    xs, gate_in, bc_in, dt_in, placement, lengths,
    conv_x, conv_bc, a_log, dt_bias, d_skip, norm_gain, *, full_inner,
):
    shards = lax.axis_size("seq")
    mine = lax.axis_index("seq")
    rows, inner = xs.shape
    heads = a_log.shape[0]
    head_dim = inner // heads
    per = rows // shards
    width = conv_x.shape[0]
    place = placement[None, :]
    quarter = bc_in.shape[1] // lax.axis_size("head")
    bc_own = lax.dynamic_slice_in_dim(bc_in, lax.axis_index("head") * quarter, quarter, 1)
    spare = jnp.zeros((rows, LANES - heads - quarter), BF16)
    small = jnp.concatenate([dt_in, spare, bc_own], 1)

    arrived, tails, gate = move_rows(place, xs, small, gate_in, width, heads)
    tails = tails.reshape(tails.shape[0], -1, LANES)
    bc = tails[:, :, LANES - quarter :].transpose(1, 0, 2).reshape(tails.shape[1], -1)
    starts = jnp.concatenate(
        [jnp.cumsum(lengths) - lengths, jnp.asarray(mine * rows, jnp.int32)[None]]
    )
    taps = jnp.concatenate([conv_x, conv_bc], 1)
    head_rows = jnp.zeros((8, LANES), F32).at[0, :heads].set(a_log).at[1, :heads].set(dt_bias)
    skip = jnp.broadcast_to(jnp.repeat(d_skip, head_dim)[None, :], (8, inner))
    gain = jnp.broadcast_to(norm_gain[None, :], (8, inner))
    tail = lax.dynamic_index_in_dim(tails, lax.axis_index("head"), 0, keepdims=False)
    return layer(
        starts, arrived.reshape(shards * (per + RIM), inner), bc, tail, taps, head_rows, skip,
        gain, gate, per, heads, rows, full_inner,
    )


def solution(mesh):
    in_specs = (
        P(("parts", "seq"), "head"),
        P(("parts", "seq"), "head"),
        P(("parts", "seq"), None),
        P(("parts", "seq"), "head"),
        P(("parts", "seq")),
        P("parts"),
        P(None, "head"),
        P(),
        P("head"),
        P("head"),
        P("head"),
        P("head"),
    )
    out_specs = P(("parts", "seq"), "head")

    def whole(*args):
        step = functools.partial(body, full_inner=args[0].shape[1])
        return jax.shard_map(
            step, mesh=mesh, in_specs=in_specs, out_specs=out_specs, check_vma=False
        )(*args)

    return whole
```

```python
import functools

import jax
import jax.numpy as jnp
from jax import lax
from jax.experimental import pallas as pl
from jax.experimental.pallas import tpu as pltpu
from jax.sharding import PartitionSpec as P

BLOCK = 256
LANES = 128
RIM = 8
HIGHEST = lax.Precision.HIGHEST
MESH = pl.DeviceIdType.MESH
F32 = jnp.float32
BF16 = jnp.bfloat16


def iota(shape, dim):
    return lax.broadcasted_iota(jnp.int32, shape, dim)


def dot(a, b, dims=((1,), (0,))):
    return lax.dot_general(a, b, (dims, ((), ())), preferred_element_type=F32)


def halves(value):
    high = value.astype(BF16)
    return high, (value - high.astype(F32)).astype(BF16)


def dot_left(a, b):
    high, low = halves(a)
    return dot(high, b) + dot(low, b)


def dot_right(a, b):
    high, low = halves(b)
    return dot(jnp.concatenate([a, a], 1), jnp.concatenate([high, low], 0))


def dot_turned(a, b):
    high, low = halves(b)
    dims = ((0,), (0,))
    return dot(a, high, dims) + dot(a, low, dims)


def expanded(value, heads, head_dim, width):
    head, channel = iota((LANES, width), 0), iota((LANES, width), 1)
    head = jnp.where(head < heads, head, head - LANES // 2)
    inside = (channel >= head * head_dim) & (channel < (head + 1) * head_dim)
    high, low = halves(value)
    low = pltpu.roll(low.astype(F32), LANES // 2, 1)
    lane = iota((1, LANES), 1)
    both = jnp.where(lane < LANES // 2, high.astype(F32), low)
    return dot(both.astype(BF16), inside.astype(F32).astype(BF16))


def picked(place, slot, dest, per, rim, width):
    rows = place.shape[1]
    target = lax.shift_right_logical(place, rows.bit_length() - 1)
    offset = place - dest * rows
    key = jnp.where(target == dest, slot, -1)
    if rim:
        key = jnp.where((offset < 0) & (offset >= 1 - width), offset + (width - 1 + per), key)
    return (iota((per + rim, rows), 0) == key).astype(F32).astype(BF16)


def greet(axes):
    barrier = pltpu.get_barrier_semaphore()
    for axis in axes:
        count, me = lax.axis_size(axis), lax.axis_index(axis)

        def signal(i, _, axis=axis, count=count, me=me):
            pl.semaphore_signal(
                barrier, inc=1, device_id={axis: lax.rem(me + i, count)}, device_id_type=MESH
            )
            return 0

        lax.fori_loop(1, count, signal, 0)
    pl.semaphore_wait(barrier, sum(lax.axis_size(axis) - 1 for axis in axes))


def remote(source, target, sends, receives, axis, offset):
    count, me = lax.axis_size(axis), lax.axis_index(axis)
    return pltpu.make_async_remote_copy(
        src_ref=source,
        dst_ref=target,
        send_sem=sends,
        recv_sem=receives,
        device_id={axis: lax.rem(me + offset, count)},
        device_id_type=MESH,
    )


def each(first, last, action):
    def once(i, _):
        action(i)
        return 0

    lax.fori_loop(first, last, once, 0)


def move_step(
    width, heads, place_ref, x_ref, small_ref, gate_ref, arrived_ref, tails_ref, gate_in,
    x_send, small_send, gate_send, x_sems, small_sems, tail_sems, gate_copy,
):
    shards, peers = lax.axis_size("seq"), lax.axis_size("head")
    me, own = lax.axis_index("seq"), lax.axis_index("head")
    rows = place_ref.shape[1]
    per = rows // shards
    greet(("seq", "head"))
    place = place_ref[0:1, :]
    groups = -(-shards // 16) * 16
    target = lax.shift_right_logical(place, rows.bit_length() - 1)
    chosen = iota((groups, rows), 0) == target
    before = (iota((rows, rows), 0) < iota((rows, rows), 1)).astype(F32).astype(BF16)
    counts = dot(chosen.astype(F32).astype(BF16), before)
    slot = jnp.sum(jnp.where(chosen, counts, 0.0), axis=0, keepdims=True).astype(jnp.int32)
    local = place & (rows - 1)
    line = iota((LANES, rows), 0)
    digits = jnp.where(line == heads, local >> 5, jnp.where(line == heads + 1, local & 31, 0))
    digits = digits.astype(F32).astype(BF16)

    def x_copy(i):
        return remote(
            x_send.at[i], arrived_ref.at[me], x_sems.at[0, i], x_sems.at[1, i], "seq", i
        )

    def small_copy(i):
        return remote(
            small_send.at[i], tails_ref.at[own, me], small_sems.at[0, i], small_sems.at[1, i], "seq", i
        )

    def tail_copy(i):
        return remote(
            tails_ref.at[own], tails_ref.at[own], tail_sems.at[0, i], tail_sems.at[1, i], "head", i
        )

    def small_step(i, _):
        pick = picked(place, slot, lax.rem(me + i, shards), per, RIM, width)
        values = dot(pick, small_ref[...]) + dot(pick, digits, ((1,), (1,)))
        small_send[i] = values.astype(BF16)
        return 0

    def x_step(i, _):
        pick = picked(place, slot, lax.rem(me + i, shards), per, RIM, width)
        x_send[i] = dot(pick, x_ref[...]).astype(BF16)

        @pl.when(i > 1)
        def _():
            x_copy(i - 1).start()

        return 0

    lax.fori_loop(0, shards, small_step, 0)
    lax.fori_loop(1, 2, x_step, 0)
    each(1, shards, lambda i: small_copy(i).start())
    lax.fori_loop(2, shards, x_step, 0)
    tails_ref[own, me] = small_send[0]
    pick = picked(place, slot, me, per, RIM, width)
    arrived_ref[me] = dot(pick, x_ref[...]).astype(BF16)
    x_copy(shards - 1).start()

    def gate_step(i, _):
        pick = picked(place, slot, lax.rem(me + i, shards), per, 0, width)
        gate_send[i] = dot(pick, gate_ref[...]).astype(BF16)

        @pl.when(i > 1)
        def _():
            gate_copy(i - 1).start()

        return 0

    lax.fori_loop(1, shards, gate_step, 0)
    gate_in[me] = dot(picked(place, slot, me, per, 0, width), gate_ref[...]).astype(BF16)
    gate_copy(shards - 1).start()
    each(1, shards, lambda i: small_copy(i).wait())
    each(1, peers, lambda i: tail_copy(i).start())
    each(1, peers, lambda i: tail_copy(i).wait())


def doc_at(starts, position):
    total = jnp.where(starts[0] <= position, 1, 0)
    for start in starts[1:]:
        total = total + jnp.where(start <= position, 1, 0)
    return total


def starts_of(length_ref):
    starts = [jnp.int32(0)]
    for j in range(length_ref.shape[0] - 1):
        starts.append(starts[-1] + length_ref[j])
    return starts


def head_row(ref):
    lane = iota((8, LANES), 1)
    row = jnp.zeros((8, LANES), F32)
    for head in range(ref.shape[0]):
        row = jnp.where(lane == head, ref[head], row)
    return row


def scan_step(
    chunk, base, heads, length_ref, arrived_ref, bc_ref, tail_ref, conv_x_ref, conv_bc_ref,
    a_log_ref, dt_bias_ref, d_skip_ref,
    y_ref, query_ref, carry_ref, slot_ref, state_ref, total_ref,
):
    width = conv_x_ref.shape[0]
    inner = y_ref.shape[1]
    head_dim = inner // heads
    rows_in = bc_ref.shape[0]
    starts = starts_of(length_ref)
    origin = base + chunk * BLOCK
    here = pl.ds(pl.multiple_of(chunk * BLOCK, BLOCK), BLOCK)

    wanted = iota((BLOCK + RIM, rows_in), 0) + (chunk * BLOCK - RIM)
    pick = (wanted == slot_ref[0:1, :]).astype(F32).astype(BF16)
    column = iota((BLOCK, 1), 0) + origin
    docs = doc_at(starts, column)
    matches = [None] + [
        (doc_at(starts, column - lag) == docs) & (column >= lag) for lag in range(1, width)
    ]

    def convolved(packed, taps_ref):
        total = taps_ref[0:1, :] * packed[RIM:, :]
        for lag in range(1, width):
            part = taps_ref[lag : lag + 1, :] * packed[RIM - lag : RIM - lag + BLOCK, :]
            total = total + jnp.where(matches[lag], part, 0.0)
        return (total * jax.nn.sigmoid(total)).astype(BF16)

    x = convolved(dot(pick, arrived_ref[...].reshape(rows_in, inner)), conv_x_ref)
    both = convolved(dot(pick, bc_ref[...]), conv_bc_ref)
    keys, query = both[:, :LANES], both[:, LANES:]
    query_ref[here, :] = query
    raw = dot(pick, tail_ref[...])[RIM:, :]
    raw = raw + head_row(dt_bias_ref)[0:1, :]
    lane = iota((1, LANES), 1)
    step = jnp.maximum(raw, 0.0) + jnp.log1p(jnp.exp(-jnp.abs(raw)))
    step = jnp.where(lane < heads, step, 0.0)
    rate = jnp.exp(head_row(a_log_ref)[0:1, :])
    decay = -rate * step
    lower = iota((BLOCK, BLOCK), 0) >= iota((BLOCK, BLOCK), 1)
    sums = jnp.dot(lower.astype(F32), decay, precision=HIGHEST, preferred_element_type=F32)
    sums_t = sums.T
    step_t = step.T
    docs_row = doc_at(starts, iota((1, BLOCK), 1) + origin)
    linked = lower & (docs == docs_row)
    scores = jnp.where(linked, dot(query, keys, ((1,), (1,))), 0.0)
    doc_before = doc_at(starts, origin - 1)
    doc_before = jnp.where(origin > 0, doc_before, 0)
    doc_base = jnp.where(base > 0, doc_at(starts, base - 1), 0)
    doc_last = doc_at(starts, origin + BLOCK - 1)
    carried = jnp.where(docs == doc_before, jnp.exp(sums), 0.0)
    last = sums[BLOCK - 1 : BLOCK, :]
    closing = jnp.where(docs == doc_last, jnp.exp(jnp.minimum(last - sums, 0.0)), 0.0) * step
    before = total_ref[0:1, :]
    carry_ref[here, :] = jnp.where(docs == doc_base, jnp.exp(before + sums), 0.0)
    total_ref[...] = jnp.broadcast_to(before + last, total_ref.shape)

    carried_all = expanded(carried, heads, head_dim, inner)
    state = state_ref[...]
    x32 = x.astype(F32)
    skip = expanded(head_row(d_skip_ref), heads, head_dim, inner)[0:1, :]
    y_ref[here, :] = carried_all * dot_right(query, state) + skip * x32
    weighted = expanded(closing, heads, head_dim, inner) * x32
    state_ref[...] = carried_all[BLOCK - 1 : BLOCK, :] * state + dot_turned(keys, weighted)

    for head in range(heads):
        first, end = head * head_dim, (head + 1) * head_dim
        low, high = first // LANES * LANES, -(-end // LANES) * LANES
        gap = sums[:, head : head + 1] - sums_t[head : head + 1, :]
        weight = jnp.exp(jnp.minimum(gap, 0.0)) * step_t[head : head + 1, :] * scores
        channel = iota((1, high - low), 1) + low
        own = jnp.where((channel >= first) & (channel < end), x32[:, low:high], 0.0).astype(BF16)
        y_ref[here, low:high] += dot_left(weight, own)


def start_step(per, heads, tail_ref, slot_ref, gate_slot_ref):
    shards = lax.axis_size("seq")
    block = per + RIM
    lane, row = iota((16, LANES), 1), iota((16, LANES), 0)
    factor = jnp.where(lane == heads, 32.0, jnp.where(lane == heads + 1, 1.0, 0.0))
    factor = jnp.where(row == 0, factor, 0.0).astype(BF16)
    place = dot(factor, tail_ref[...], ((1,), (1,)))[0:8, :].astype(jnp.int32)
    within = iota((8, shards * block), 1) % block
    slot_ref[...] = jnp.where(within >= per, place - per * shards, place)
    for source in range(shards):
        gate_slot_ref[source] = place[:, source * block : source * block + per]


def layer_kernel(
    per, heads, full_inner, length_ref, a_log_ref, dt_bias_ref, d_skip_ref, place_ref, x_ref,
    small_ref, gate_ref, conv_x_ref, conv_bc_ref, gain_ref, out_ref,
    arrived_ref, tails_ref, x_send, small_send, gate_send, bc_ref, tail_ref,
    y_ref, gate_sum, query_ref, carry_ref, slot_ref, gate_slot_ref, state_ref, total_ref,
    gate_in, came, onward, incoming, squares,
    x_sems, small_sems, tail_sems, gate_sems, state_sems, square_sems,
):
    shards, peers = lax.axis_size("seq"), lax.axis_size("head")
    me, own = lax.axis_index("seq"), lax.axis_index("head")
    step = pl.program_id(0)
    rows, inner = y_ref.shape
    chunks = rows // BLOCK
    head_dim = inner // heads
    pieces, _, wide = came.shape
    width = conv_x_ref.shape[0]
    block = per + RIM
    quarter = bc_ref.shape[1] // peers

    def gate_copy(i):
        return remote(
            gate_send.at[i], gate_in.at[me], gate_sems.at[0, i], gate_sems.at[1, i], "seq", i
        )

    def state_copy(piece):
        return remote(
            onward.at[piece], came.at[piece], state_sems.at[0, piece], state_sems.at[1, piece], "seq", 1
        )

    def square_copy(chunk, i):
        return remote(
            squares.at[own, chunk], squares.at[own, chunk],
            square_sems.at[0, chunk, i], square_sems.at[1, chunk, i], "head", i,
        )

    @pl.when(step == 0)
    def _():
        move_step(
            width, heads, place_ref, x_ref, small_ref, gate_ref, arrived_ref, tails_ref, gate_in,
            x_send, small_send, gate_send, x_sems, small_sems, tail_sems, gate_copy,
        )
        for source in range(shards):
            here = slice(source * block, (source + 1) * block)
            parts = [tails_ref[peer, source][:, LANES - quarter :] for peer in range(peers)]
            bc_ref[here, :] = jnp.concatenate(parts, 1)
            tail_ref[here, :] = tails_ref[own, source]
        start_step(per, heads, tail_ref, slot_ref, gate_slot_ref)
        state_ref[...] = jnp.zeros_like(state_ref)
        total_ref[...] = jnp.zeros_like(total_ref)
        each(
            1,
            shards,
            lambda i: remote(
                x_send.at[i], arrived_ref.at[me], x_sems.at[0, i], x_sems.at[1, i], "seq", i
            ).wait(),
        )

    @pl.when(step < chunks)
    def _():
        scan_step(
            step, me * rows, heads, length_ref, arrived_ref, bc_ref, tail_ref, conv_x_ref,
            conv_bc_ref, a_log_ref, dt_bias_ref, d_skip_ref,
            y_ref, query_ref, carry_ref, slot_ref, state_ref, total_ref,
        )

    @pl.when(step == chunks - 1)
    def _():
        tail_rows = carry_ref[rows - 8 : rows, :]
        keep = expanded(tail_rows, heads, head_dim, inner)[7:8, :]
        for piece in range(pieces):
            span = slice(piece * wide, (piece + 1) * wide)

            @pl.when(me > 0)
            def _():
                state_copy(piece).wait_recv()
                incoming[:, span] = came[piece].astype(F32)

            @pl.when(me == 0)
            def _():
                incoming[:, span] = jnp.zeros((LANES, wide), F32)

            passed = keep[:, span] * incoming[:, span] + state_ref[:, span]
            onward[piece] = passed.astype(BF16)
            if piece > 0:

                @pl.when(me < shards - 1)
                def _():
                    state_copy(piece - 1).start()

        state_ref[...] = incoming[...]

        @pl.when(me < shards - 1)
        def _():
            state_copy(pieces - 1).start()
            for piece in range(pieces):
                state_copy(piece).wait_send()

        def add_state(chunk):
            here = pl.ds(pl.multiple_of(chunk * BLOCK, BLOCK), BLOCK)
            carried = expanded(carry_ref[here, :], heads, head_dim, inner)
            y_ref[here, :] += carried * dot(query_ref[here, :], state_ref[...].astype(BF16))

        each(0, chunks, add_state)

        def unsort(i, fresh):
            source = lax.rem(me - i + shards, shards)

            def one(chunk):
                here = pl.ds(pl.multiple_of(chunk * BLOCK, BLOCK), BLOCK)
                wanted = iota((BLOCK, per), 0) + chunk * BLOCK
                pick = (wanted == gate_slot_ref[source, 0:1, :]).astype(F32).astype(BF16)
                part = dot(pick, gate_in[source])
                gate_sum[here, :] = part if fresh else gate_sum[here, :] + part

            each(0, chunks, one)

        unsort(0, True)

        def unsort_next(i):
            gate_copy(i).wait()
            unsort(i, False)

        each(1, shards, unsort_next)

    @pl.when((step > chunks) & (step <= 2 * chunks))
    def _():
        each(1, peers, lambda i: square_copy(step - chunks - 1, i).start())

    @pl.when((step >= chunks) & (step < 2 * chunks))
    def _():
        chunk = step - chunks
        here = pl.ds(pl.multiple_of(chunk * BLOCK, BLOCK), BLOCK)
        gate = gate_sum[here, :]
        y = y_ref[here, :]
        gated = y * (gate * jax.nn.sigmoid(gate))
        y_ref[here, :] = gated
        total = jnp.sum(gated * gated, axis=1, keepdims=True)
        squares[own, chunk] = jnp.broadcast_to(total, (BLOCK, LANES)).T[0:8, :]

    @pl.when(step >= 2 * chunks)
    def _():
        chunk = step - 2 * chunks
        here = pl.ds(pl.multiple_of(chunk * BLOCK, BLOCK), BLOCK)
        each(1, peers, lambda i: square_copy(chunk, i).wait())
        total = squares[0, chunk]
        for peer in range(1, peers):
            total = total + squares[peer, chunk]
        scale = lax.rsqrt(total / full_inner + 1e-05)
        scale = jnp.concatenate([scale] * (LANES // 8), 0).T[:, 0:1]
        out_ref[...] = (y_ref[here, :] * scale * gain_ref[0:1, :]).astype(BF16)


def layer(lengths, a_log, dt_bias, d_skip, place, xs, small, gate, conv_x, conv_bc, gain, full_inner):
    shards, peers = lax.axis_size("seq"), lax.axis_size("head")
    rows, inner = xs.shape
    heads = a_log.shape[0]
    per = rows // shards
    block = per + RIM
    chunks = rows // BLOCK
    wide = 2 * LANES
    pieces = inner // wide
    vmem = pl.BlockSpec(memory_space=pltpu.VMEM)
    return pl.pallas_call(
        functools.partial(layer_kernel, per, heads, full_inner),
        grid=(3 * chunks,),
        in_specs=[pl.BlockSpec(memory_space=pltpu.SMEM)] * 4 + [vmem] * 7,
        out_specs=pl.BlockSpec((BLOCK, inner), lambda k: (jnp.maximum(k - 2 * chunks, 0), 0)),
        out_shape=jax.ShapeDtypeStruct((rows, inner), BF16),
        scratch_shapes=[
            pltpu.VMEM((shards, block, inner), BF16),
            pltpu.VMEM((peers, shards, block, LANES), BF16),
            pltpu.VMEM((shards, block, inner), BF16),
            pltpu.VMEM((shards, block, LANES), BF16),
            pltpu.VMEM((shards, per, inner), BF16),
            pltpu.VMEM((shards * block, conv_bc.shape[1]), BF16),
            pltpu.VMEM((shards * block, LANES), BF16),
            pltpu.VMEM((rows, inner), F32),
            pltpu.VMEM((rows, inner), F32),
            pltpu.VMEM((rows, LANES), BF16),
            pltpu.VMEM((rows, LANES), F32),
            pltpu.VMEM((8, shards * block), jnp.int32),
            pltpu.VMEM((shards, 8, per), jnp.int32),
            pltpu.VMEM((LANES, inner), F32),
            pltpu.VMEM((8, LANES), F32),
            pltpu.VMEM((shards, per, inner), BF16),
            pltpu.VMEM((pieces, LANES, wide), BF16),
            pltpu.VMEM((pieces, LANES, wide), BF16),
            pltpu.VMEM((LANES, inner), F32),
            pltpu.VMEM((peers, chunks, 8, BLOCK), F32),
            pltpu.SemaphoreType.DMA((2, shards)),
            pltpu.SemaphoreType.DMA((2, shards)),
            pltpu.SemaphoreType.DMA((2, peers)),
            pltpu.SemaphoreType.DMA((2, shards)),
            pltpu.SemaphoreType.DMA((2, pieces)),
            pltpu.SemaphoreType.DMA((2, chunks, peers)),
        ],
        compiler_params=pltpu.CompilerParams(
            collective_id=0, has_side_effects=True, vmem_limit_bytes=60 << 20
        ),
    )(lengths, a_log, dt_bias, d_skip, place, xs, small, gate, conv_x, conv_bc, gain)


def body(
    xs, gate_in, bc_in, dt_in, placement, lengths,
    conv_x, conv_bc, a_log, dt_bias, d_skip, norm_gain, *, full_inner,
):
    rows = xs.shape[0]
    heads = a_log.shape[0]
    quarter = bc_in.shape[1] // lax.axis_size("head")
    bc_own = lax.dynamic_slice_in_dim(bc_in, lax.axis_index("head") * quarter, quarter, 1)
    spare = jnp.zeros((rows, LANES - heads - quarter), BF16)
    small = jnp.concatenate([dt_in, spare, bc_own], 1)
    return layer(
        lengths, a_log, dt_bias, d_skip, placement[None, :], xs, small, gate_in, conv_x, conv_bc,
        norm_gain[None, :], full_inner,
    )


def solution(mesh):
    in_specs = (
        P(("parts", "seq"), "head"),
        P(("parts", "seq"), "head"),
        P(("parts", "seq"), None),
        P(("parts", "seq"), "head"),
        P(("parts", "seq")),
        P("parts"),
        P(None, "head"),
        P(),
        P("head"),
        P("head"),
        P("head"),
        P("head"),
    )
    out_specs = P(("parts", "seq"), "head")

    def whole(*args):
        step = functools.partial(body, full_inner=args[0].shape[1])
        return jax.shard_map(
            step, mesh=mesh, in_specs=in_specs, out_specs=out_specs, check_vma=False
        )(*args)

    return whole
```
